256 devices in a mesh: gx: 64 (over z, y, x_hi), gy: 4 (over x_lo, core).
Axes of the slice: x: 4 (x_hi: 2, x_lo: 2; x = x_hi * 2 + x_lo), y: 4, z: 8, core: 2. Of those that a mesh axis runs over, the one named last changes fastest.
Arguments:
- pressure: float32 [256, 256, 128], P('gx', 'gy'), may hold values from 0.5 to 2
- sat_water: float32 [256, 256, 128], P('gx', 'gy'), may hold values from 0.15 to 0.45
- sat_gas: float32 [256, 256, 128], P('gx', 'gy'), may hold values from 0.05 to 0.35
- pore_volume: float32 [256, 256, 128], P('gx', 'gy'), may hold values from 0.05 to 0.5
- mass_old: float32 [3, 256, 256, 128], P(None, 'gx', 'gy'), may hold values from -1.5 to 1.5
- transmissibility: float32 [3, 256, 256, 128], P(None, 'gx', 'gy'), may hold values from 0.1 to 3
- upwind: int32 [3, 3, 256, 256, 128], P(None, None, 'gx', 'gy'), may hold values from 0 to 1
Outputs:
- residual: float32 [3, 256, 256, 128], P(None, 'gx', 'gy')
- diag_block: float32 [9, 256, 256, 128], P(None, 'gx', 'gy')
- lower_block: float32 [3, 9, 256, 256, 128], P(None, None, 'gx', 'gy')
- upper_block: float32 [3, 9, 256, 256, 128], P(None, None, 'gx', 'gy')
- pressure_rows: float32 [7, 256, 256, 128], P(None, 'gx', 'gy')
- prolongator: float32 [7, 256, 256, 128], P(None, 'gx', 'gy')
- coarse_rhs: float32 [128, 128, 128], P('gx', 'gy')
The draws below stay inside these ranges and needn't reach their ends.
All inputs are finite; a program needn't handle non-finite values.
Results may differ from the reference program's by a relative error of at most 0.0001.
Values sent between devices are 32-bit elements; how exact they have to be, the bound alone decides.
No kernel may reach another device: no remote copies, remote signals or barrier semaphores. Data moves between devices by JAX's collectives and lax.ppermute only.
A program may use at most 64 MiB of HBM per device.

```python
import math
import jax
import jax.numpy as jnp
from jax import lax

NZ = 128
NX = 256
NY = 256


def touch_ends(values, key, smallest, largest):
    longest = values.shape.index(max(values.shape))
    spots = []
    for shift in (0, 1):
        where = [jax.random.randint(jax.random.fold_in(key, axis), (), 0, length) for axis, length in enumerate(values.shape)]
        where[longest] = (where[longest] + shift) % values.shape[longest]
        spots.append(tuple(where))
    return values.at[spots[0]].set(smallest).at[spots[1]].set(largest)


def level_of(own_key, extent, shards, least, largest):
    loudness = 1.0
    for position, parts in shards:
        draws = jax.random.uniform(jax.random.fold_in(jax.random.fold_in(own_key, 6), position), (parts,), jnp.float32, least / len(shards), largest / len(shards))
        loudness = loudness * jnp.repeat(jnp.exp(draws), extent[position] // parts).reshape((-1,) + (1,) * (len(extent) - 1 - position))
    return loudness


def centred(stream_key, extent, spread, most, split=(), kind=jnp.bfloat16):
    values = jax.random.normal(stream_key, extent, jnp.float32) * spread
    if len(split) > 0:
        values = level_of(stream_key, extent, split, -0.22, 0.18) * values
    return jnp.clip(values, min=-most, max=most).astype(kind)


def setup_inputs(seed: int = 0) -> dict:
    key_of = jax.random.split(jax.random.key(seed), 8)
    pressure = jnp.clip(0.5 + 1.5 * jax.random.uniform(key_of[0], (NX, NY, NZ), jnp.float32) ** level_of(key_of[0], (NX, NY, NZ), ((0, 64), (1, 4)), -0.2, 0.2), 0.5, 2.0)
    sat_water = jnp.clip(0.15 + 0.29999998 * jax.random.uniform(key_of[1], (NX, NY, NZ), jnp.float32) ** level_of(key_of[1], (NX, NY, NZ), ((0, 64), (1, 4)), -0.2, 0.2), 0.15, 0.45)
    sat_gas = jnp.clip(0.05 + 0.29999999 * jax.random.uniform(key_of[2], (NX, NY, NZ), jnp.float32) ** level_of(key_of[2], (NX, NY, NZ), ((0, 64), (1, 4)), -0.2, 0.2), 0.05, 0.35)
    pore_volume = jnp.clip(jnp.exp(math.log(0.5) - 2.3025851 * jax.random.uniform(key_of[3], (NX, NY, NZ), jnp.float32) ** level_of(key_of[3], (NX, NY, NZ), ((0, 64), (1, 4)), -0.2, 0.2)), 0.05, 0.5)
    mass_old = centred(key_of[4], (3, NX, NY, NZ), 0.1, 1.5, ((1, 64), (2, 4)), jnp.float32)
    transmissibility = jnp.clip(jnp.exp(math.log(3.0) - 3.4011974 * jax.random.uniform(key_of[5], (3, NX, NY, NZ), jnp.float32) ** level_of(key_of[5], (3, NX, NY, NZ), ((1, 64), (2, 4)), -0.2, 0.2)), 0.1, 3.0)
    upwind = touch_ends(jax.random.randint(key_of[6], (3, 3, NX, NY, NZ), 0, 2), jax.random.fold_in(key_of[6], 1), 0, 1).astype(jnp.int32)
    return {"pressure": pressure, "sat_water": sat_water, "sat_gas": sat_gas, "pore_volume": pore_volume, "mass_old": mass_old, "transmissibility": transmissibility, "upwind": upwind}


comp_water = 0.05
comp_oil = 0.1
rock_comp = 0.02
gas_ratio = 0.3
visc_water = 0.5
visc_oil = 2.0
visc_gas = 0.2
head_flat = (0.0, 0.0, 0.0)
head_depth = (0.1, 0.08, 0.02)
time_step = 0.5
damping = 2.0 / 3.0

def volumes(states):
    press = states[0]
    water = states[1]
    gas_sat = states[2]
    oil_sat = 1.0 - water - gas_sat
    b_water = 1.0 + comp_water * press
    b_oil = 1.0 + comp_oil * press
    return (press, water, gas_sat, oil_sat, b_water, b_oil, press)

def mobility(states):
    press, water, gas_sat, oil_sat, b_water, b_oil, b_gas = volumes(states)
    moving = jnp.stack([water * water * b_water / visc_water, oil_sat * oil_sat * b_oil / visc_oil, gas_sat * gas_sat * b_gas / visc_gas])
    return (moving, gas_ratio * press)

def face_flux(lower_state, upper_state, trans, upwind, head):
    mob_lower, solved_lower = mobility(lower_state)
    mob_upper, solved_upper = mobility(upper_state)
    chosen = upwind * mob_lower + (1.0 - upwind) * mob_upper
    drop = lower_state[0] - upper_state[0]
    heads = jnp.array(head, jnp.float32).reshape(3, 1, 1, 1)
    phases = trans[None] * chosen * (drop[None] + heads)
    solved = upwind[1] * solved_lower + (1.0 - upwind[1]) * solved_upper
    return jnp.stack([phases[0], phases[1], phases[2] + solved * phases[1]])

def unit_rows(template):
    return [jnp.stack([jnp.ones_like(template[0]) if column == row else jnp.zeros_like(template[0]) for column in range(3)]) for row in range(3)]

def face_terms(lower_state, upper_state, trans, upwind, head):
    fluxes, pullback = jax.vjp(lambda first, second: face_flux(first, second, trans, upwind, head), lower_state, upper_state)
    by_lower = []
    by_upper = []
    for cotangent in unit_rows(fluxes):
        wrt_lower, wrt_upper = pullback(cotangent)
        by_lower.append(wrt_lower)
        by_upper.append(wrt_upper)
    return (fluxes, jnp.concatenate(by_lower, 0), jnp.concatenate(by_upper, 0))

def accumulate(states, pore_volume):
    press, water, gas_sat, oil_sat, b_water, b_oil, b_gas = volumes(states)
    porosity = pore_volume * (1.0 + rock_comp * press)
    return jnp.stack([porosity * b_water * water, porosity * b_oil * oil_sat, porosity * (b_gas * gas_sat + gas_ratio * press * b_oil * oil_sat)])

def accumulation_terms(states, pore_volume):
    masses, pullback = jax.vjp(lambda first: accumulate(first, pore_volume), states)
    rows = [pullback(cotangent)[0] for cotangent in unit_rows(masses)]
    return (masses, jnp.concatenate(rows, 0))

def impes_weights(states):
    press, water, gas_sat, oil_sat, b_water, b_oil, b_gas = volumes(states)
    return jnp.stack([1.0 / b_water, 1.0 / b_oil - gas_ratio, 1.0 / b_gas])

def cut_layer(field, dimension, first_index, last_index):
    return lax.slice_in_dim(field, first_index, last_index, axis=dimension)

def raise_up(field, upper_face, dimension):
    count = field.shape[dimension]
    return jnp.concatenate([cut_layer(field, dimension, 1, count), upper_face], dimension)

def sink_down(field, lower_face, dimension):
    count = field.shape[dimension]
    return jnp.concatenate([lower_face, cut_layer(field, dimension, 0, count - 1)], dimension)

def face_field(states, below, dimension, start, trans, upwind, head):
    lower_state = sink_down(states, below, dimension)
    positions = start + lax.broadcasted_iota(jnp.int32, trans.shape, dimension - 1)
    trans_live = jnp.where(positions > 0, trans, jnp.zeros_like(trans))
    return face_terms(lower_state, states, trans_live, upwind, head)

def assemble(masses, acc_block, mass_old, faces_all, tops_all):
    residual = (masses - mass_old) / time_step
    diagonal = acc_block / time_step
    lowers = []
    uppers = []
    for direction in range(3):
        fluxes, by_lower, by_upper = faces_all[direction]
        flux_top, lower_top, upper_top = tops_all[direction]
        dimension = direction + 1
        residual = residual - fluxes + raise_up(fluxes, flux_top, dimension)
        diagonal = diagonal - by_upper + raise_up(by_lower, lower_top, dimension)
        lowers.append(-by_lower)
        uppers.append(raise_up(by_upper, upper_top, dimension))
    return (residual, diagonal, lowers, uppers)

def pressure_section(weight, acc_block, diagonal, lowers, uppers, odd_x, odd_y):

    def column(block):
        return lax.optimization_barrier(jnp.sum(weight * block[0::3], axis=0))
    press_diag = column(diagonal)
    press_lower = [column(block) for block in lowers]
    press_upper = [column(block) for block in uppers]
    accum = column(acc_block) / time_step
    divisor = jnp.abs(press_diag) + accum
    for entry in press_lower + press_upper:
        divisor = divisor + jnp.abs(entry)
    scale = damping / divisor
    nothing = jnp.zeros_like(odd_x)
    same_lower = [odd_x, odd_y, nothing]
    same_upper = [1.0 - odd_x, 1.0 - odd_y, nothing]
    inside = press_diag
    for direction in range(3):
        inside = inside + same_lower[direction] * press_lower[direction] + same_upper[direction] * press_upper[direction]
    own_weight = 1.0 - scale * inside
    near_lower = [-scale * press_lower[direction] * (1.0 - same_lower[direction]) for direction in range(3)]
    near_upper = [-scale * press_upper[direction] * (1.0 - same_upper[direction]) for direction in range(3)]
    rows_out = jnp.stack([press_diag] + press_lower + press_upper)
    prolong = jnp.stack([own_weight] + near_lower + near_upper)
    return (rows_out, prolong)

def contributions(prolong, residual, weight):
    reduced = lax.optimization_barrier(jnp.sum(weight * residual, axis=0))
    shares = prolong * reduced[None]
    layer_z = jnp.zeros_like(reduced[:, :, 0:1])
    local_sum = shares[0] + raise_up(shares[3], layer_z, 2) + sink_down(shares[6], layer_z, 2)
    sideways = jnp.stack([shares[1], shares[4], shares[2], shares[5]])
    return (local_sum, sideways)

def block_sum(field):
    span_a, span_b, span_c = field.shape[-3:]
    shaped = field.reshape(field.shape[:-3] + (span_a // 2, 2, span_b // 2, 2, span_c))
    return lax.optimization_barrier(jnp.sum(shaped, axis=(-4, -2)))

def reference(pressure, sat_water, sat_gas, pore_volume, mass_old, transmissibility, upwind):
    states = jnp.stack([pressure, sat_water, sat_gas])
    masses, acc_block = accumulation_terms(states, pore_volume)
    weight = impes_weights(states)
    flags = upwind.astype(jnp.float32)
    faces_all = []
    tops_all = []
    for direction in range(3):
        dimension = direction + 1
        below = jnp.zeros_like(cut_layer(states, dimension, 0, 1))
        head = head_depth if direction == 2 else head_flat
        faces_all.append(face_field(states, below, dimension, 0, transmissibility[direction], flags[direction], head))
        zero_nine = jnp.zeros_like(cut_layer(acc_block, dimension, 0, 1))
        tops_all.append((below, zero_nine, zero_nine))
    residual, diagonal, lowers, uppers = assemble(masses, acc_block, mass_old, faces_all, tops_all)
    odd_x = (lax.broadcasted_iota(jnp.int32, pressure.shape, 0) % 2).astype(jnp.float32)
    odd_y = (lax.broadcasted_iota(jnp.int32, pressure.shape, 1) % 2).astype(jnp.float32)
    rows_out, prolong = pressure_section(weight, acc_block, diagonal, lowers, uppers, odd_x, odd_y)
    local_sum, sideways = contributions(prolong, residual, weight)
    edge_x = jnp.zeros_like(local_sum[0:1])
    edge_y = jnp.zeros_like(local_sum[:, 0:1])
    total = local_sum + raise_up(sideways[0], edge_x, 0) + sink_down(sideways[1], edge_x, 0)
    total = total + raise_up(sideways[2], edge_y, 1) + sink_down(sideways[3], edge_y, 1)
    coarse = block_sum(total)
    return (residual, diagonal, jnp.stack(lowers), jnp.stack(uppers), rows_out, prolong, coarse)
```

```python
import jax
import jax.numpy as jnp
from jax import lax
from jax.experimental import pallas as pl
from jax.experimental.pallas import tpu as pltpu
from jax.sharding import PartitionSpec as P

comp_water = 0.05
comp_oil = 0.1
rock_comp = 0.02
gas_ratio = 0.3
head_flat = (0.0, 0.0, 0.0)
head_depth = (0.1, 0.08, 0.02)
damping = 2.0 / 3.0
f32 = jnp.float32

distinct = 7
entry_of = (0, 1, -1, 2, 3, 3, 4, 5, 6)


def mobility_set(press, water, gas_sat):
    oil_sat = 1.0 - water - gas_sat
    b_water = 1.0 + comp_water * press
    b_oil = 1.0 + comp_oil * press
    water_sq = water * water
    oil_sq = oil_sat * oil_sat
    gas_sq = 5.0 * (gas_sat * gas_sat)
    return {
        "p": press,
        "rs": gas_ratio * press,
        "value": (2.0 * (water_sq * b_water), 0.5 * (oil_sq * b_oil), gas_sq * press),
        "by_p": ((2.0 * comp_water) * water_sq, (0.5 * comp_oil) * oil_sq, gas_sq),
        "by_s": (4.0 * (water * b_water), -(oil_sat * b_oil), 10.0 * (gas_sat * press)),
    }


def face(low, high, trans, flags, head):
    drop = low["p"] - high["p"]
    flux, lp, ls, hp, hs = [], [], [], [], []
    for a in range(3):
        push = trans * (drop + head[a]) if head[a] != 0.0 else trans * drop
        chosen = jnp.where(flags[a], low["value"][a], high["value"][a])
        moved = trans * chosen
        push_low = jnp.where(flags[a], push, 0.0)
        push_high = jnp.where(flags[a], 0.0, push)
        flux.append(push * chosen)
        lp.append(push_low * low["by_p"][a] + moved)
        hp.append(push_high * high["by_p"][a] - moved)
        ls.append(push_low * low["by_s"][a])
        hs.append(push_high * high["by_s"][a])
    solved = jnp.where(flags[1], low["rs"], high["rs"])
    extra = gas_ratio * flux[1]
    by_low = [
        lp[0], ls[0], lp[1], ls[1],
        lp[2] + solved * lp[1] + jnp.where(flags[1], extra, 0.0),
        solved * ls[1],
        ls[2] + solved * ls[1],
    ]
    by_high = [
        hp[0], hs[0], hp[1], hs[1],
        hp[2] + solved * hp[1] + jnp.where(flags[1], 0.0, extra),
        solved * hs[1],
        hs[2] + solved * hs[1],
    ]
    return [flux[0], flux[1], flux[2] + solved * flux[1]], by_low, by_high


def accumulation(press, water, gas_sat, pore):
    oil_sat = 1.0 - water - gas_sat
    b_water = 1.0 + comp_water * press
    b_oil = 1.0 + comp_oil * press
    porosity = pore * (1.0 + rock_comp * press)
    by_rock = rock_comp * pore
    in_water = b_water * water
    in_oil = b_oil * oil_sat
    solved = gas_ratio * press
    in_gas = press * gas_sat + solved * in_oil
    masses = [porosity * in_water, porosity * in_oil, porosity * in_gas]
    oil_by_s = -(porosity * b_oil)
    gas_by_water = solved * oil_by_s
    block = [
        by_rock * in_water + porosity * (comp_water * water),
        porosity * b_water,
        by_rock * in_oil + porosity * (comp_oil * oil_sat),
        oil_by_s,
        by_rock * in_gas
        + porosity * (gas_sat + gas_ratio * in_oil + (gas_ratio * comp_oil) * (press * oil_sat)),
        gas_by_water,
        porosity * press + gas_by_water,
    ]
    return masses, block


def weights_of(press):
    return (
        1.0 / (1.0 + comp_water * press),
        1.0 / (1.0 + comp_oil * press) - gas_ratio,
        1.0 / press,
    )


def column(weight, block):
    return weight[0] * block[0] + weight[1] * block[2] + weight[2] * block[4]


def prolong_of(cols, accum, x_odd, row_odd):
    divisor = jnp.abs(cols[0]) + accum
    for entry in cols[1:]:
        divisor = divisor + jnp.abs(entry)
    scale = damping / divisor
    same_x, far_x = (cols[1], cols[4]) if x_odd else (cols[4], cols[1])
    inside = cols[0] + same_x + jnp.where(row_odd, cols[2], cols[5])
    far_x = -scale * far_x
    nothing = jnp.zeros_like(far_x)
    return [
        1.0 - scale * inside,
        nothing if x_odd else far_x,
        jnp.where(row_odd, 0.0, -scale * cols[2]),
        -scale * cols[3],
        far_x if x_odd else nothing,
        jnp.where(row_odd, -scale * cols[5], 0.0),
        -scale * cols[6],
    ]


def shares_of(weights, reduced, lanes):
    near = weights[0] * reduced
    near = near + pltpu.roll(weights[3] * reduced, lanes - 1, 1)
    near = near + pltpu.roll(weights[6] * reduced, 1, 1)
    return near, (weights[2] + weights[5]) * reduced


def pack_kernel(p_hbm, w_hbm, g_hbm, t_hbm, u_hbm, xup, xdn, yev, yod, top, bot, bot_t, bot_u, face_u, sem):
    span_x, span_y, _ = p_hbm.shape
    rows = top.shape[2]
    copies = []

    def fetch(src, dst):
        copy = pltpu.make_async_copy(src, dst, sem.at[len(copies)])
        copy.start()
        copies.append(copy)

    for k, src in enumerate((p_hbm, w_hbm, g_hbm)):
        fetch(src.at[:, pl.ds(span_y - rows, rows)], top.at[k])
        fetch(src.at[:, pl.ds(0, rows)], bot.at[k])
    fetch(t_hbm.at[1, :, pl.ds(0, rows)], bot_t)
    fetch(u_hbm.at[1, :, :, pl.ds(0, rows)], bot_u)
    fetch(t_hbm.at[0, 0], xdn.at[3])
    fetch(u_hbm.at[0, :, 0], face_u)
    for k, src in enumerate((p_hbm, w_hbm, g_hbm)):
        fetch(src.at[span_x - 1], xup.at[k])
        fetch(src.at[0], xdn.at[k])
    for copy in copies:
        copy.wait()
    at_x0 = lax.axis_index("gx") == 0
    at_y0 = lax.axis_index("gy") == 0
    even = lax.axis_index("gy") % 2 == 0
    below = [bot[k, :, 0, :] for k in range(3)]
    below.append(jnp.where(at_y0, 0.0, bot_t[:, 0, :]))
    below += [bot_u[k, :, 0, :].astype(f32) for k in range(3)]
    above = [top[k, :, rows - 1, :] for k in range(3)]
    above += [jnp.zeros_like(above[0])] * 4
    for k in range(7):
        yev[k] = jnp.where(even, above[k], below[k])
        yod[k] = jnp.where(even, below[k], above[k])
    xdn[3] = jnp.where(at_x0, 0.0, xdn[3])
    for k in range(3):
        xdn[4 + k] = face_u[k].astype(f32)


def main_kernel(
    p_ref, w_ref, g_ref, v_ref, old_ref, t_ref, u_ref, yev, yod,
    res_hbm, diag_hbm, low_hbm, up_hbm, rows_hbm, pro_hbm, part, coarse, coarse_y,
    o_res, o_diag, o_low, o_up, o_rows, o_pro, fy, edge, sem,
):
    span_x, span_y, lanes = p_ref.shape
    size = 8
    chunks = span_y // size
    gy = lax.axis_index("gy")
    even = gy % 2 == 0
    row = lax.broadcasted_iota(jnp.int32, (size, lanes), 0)
    lane = lax.broadcasted_iota(jnp.int32, (size, lanes), 1)
    row_odd = row % 2 == 1
    first_row = row == 0
    zero = jnp.zeros((size, lanes), f32)
    last_x = span_x - 1

    def halo(k, upper):
        return jnp.where(even == upper, yev[k], yod[k])

    top = [jnp.concatenate([ref[x, span_y - 1 : span_y, :] for x in range(span_x)], 0) for ref in (p_ref, w_ref, g_ref)]
    above = [halo(k, True) for k in range(7)]
    flux, by_low, by_high = face(
        mobility_set(*top), mobility_set(*above[:3]), above[3], [a > 0.5 for a in above[4:]], head_flat
    )
    for x in range(span_x):
        for k, value in enumerate(flux + by_low + by_high):
            fy[x, k, size : size + 1, :] = value[x : x + 1]
    for k in range(3):
        edge[k] = halo(k, False)

    def chunk(step, carry):
        c = chunks - 1 - step
        base = pl.multiple_of(c * size, size)
        here = pl.ds(base, size)
        before = jnp.maximum(base - 1, 0)
        bottom = c == 0
        live_y = jnp.logical_or(jnp.logical_not(first_row), gy * span_y + base > 0)
        states = [(p_ref[x, here, :], w_ref[x, here, :], g_ref[x, here, :]) for x in range(1)]
        own_next = mobility_set(*states[0])
        state_next = states[0]
        x_face = None
        for x in range(span_x):
            own, state = own_next, state_next
            weight = weights_of(state[0])
            masses, acc = accumulation(*state, v_ref[x, here, :])
            res = [2.0 * (masses[k] - old_ref[k, x, here, :]) for k in range(3)]
            accum = 2.0 * column(weight, acc)
            diag = [2.0 * entry for entry in acc]
            cols = [None] * 7

            def put(ref, direction, block, sign):
                for k in range(9):
                    value = zero if entry_of[k] < 0 else block[entry_of[k]]
                    ref[direction, k, x, here, :] = -value if sign < 0 and entry_of[k] >= 0 else value

            if x_face is not None:
                flux, by_low, by_high = x_face
                res = [a - b for a, b in zip(res, flux)]
                diag = [a - b for a, b in zip(diag, by_high)]
                put(o_low, 0, by_low, -1)
                cols[1] = -column(weight, by_low)
            if x < last_x:
                state_next = (p_ref[x + 1, here, :], w_ref[x + 1, here, :], g_ref[x + 1, here, :])
                own_next = mobility_set(*state_next)
                flags = [u_ref[0, a, x + 1, here, :] > 0 for a in range(3)]
                x_face = face(own, own_next, t_ref[0, x + 1, here, :], flags, head_flat)
                flux, by_low, by_high = x_face
                res = [a + b for a, b in zip(res, flux)]
                diag = [a + b for a, b in zip(diag, by_low)]
                put(o_up, 0, by_high, 1)
                cols[4] = column(weight, by_high)

            shifted = []
            for k, ref in enumerate((p_ref, w_ref, g_ref)):
                entering = jnp.where(bottom, edge[k, x : x + 1, :], ref[x, pl.ds(before, 1), :])
                shifted.append(jnp.where(first_row, jnp.broadcast_to(entering, (size, lanes)), pltpu.roll(state[k], 1, 0)))
            flags = [u_ref[1, a, x, here, :] > 0 for a in range(3)]
            trans = jnp.where(live_y, t_ref[1, x, here, :], 0.0)
            flux, by_low, by_high = face(mobility_set(*shifted), own, trans, flags, head_flat)
            for k, value in enumerate(flux + by_low + by_high):
                fy[x, k, 0:size, :] = value
            res = [a - b for a, b in zip(res, flux)]
            diag = [a - b for a, b in zip(diag, by_high)]
            put(o_low, 1, by_low, -1)
            cols[2] = -column(weight, by_low)
            lifted = [fy[x, k, 1 : size + 1, :] for k in range(3 + 2 * distinct)]
            for k, value in enumerate(flux + by_low + by_high):
                fy[x, k, size : size + 1, :] = value[0:1]
            flux, by_low, by_high = lifted[:3], lifted[3 : 3 + distinct], lifted[3 + distinct :]
            res = [a + b for a, b in zip(res, flux)]
            diag = [a + b for a, b in zip(diag, by_low)]
            put(o_up, 1, by_high, 1)
            cols[5] = column(weight, by_high)

            shifted = [pltpu.roll(value, 1, 1) for value in state]
            flags = [u_ref[2, a, x, here, :] > 0 for a in range(3)]
            trans = jnp.where(lane > 0, t_ref[2, x, here, :], 0.0)
            flux, by_low, by_high = face(mobility_set(*shifted), own, trans, flags, head_depth)
            res = [a - b for a, b in zip(res, flux)]
            diag = [a - b for a, b in zip(diag, by_high)]
            put(o_low, 2, by_low, -1)
            cols[3] = -column(weight, by_low)
            flux, by_low, by_high = ([pltpu.roll(v, lanes - 1, 1) for v in group] for group in (flux, by_low, by_high))
            res = [a + b for a, b in zip(res, flux)]
            diag = [a + b for a, b in zip(diag, by_low)]
            put(o_up, 2, by_high, 1)
            cols[6] = column(weight, by_high)

            if x == 0 or x == last_x:
                side = 0 if x == 0 else 1
                known = [cols[4 if x == 0 else 1], cols[2], cols[3], cols[5], cols[6]]
                for k, value in enumerate(res + diag + known + [accum]):
                    part[side, k, here, :] = value
                continue
            cols[0] = column(weight, diag)
            for k in range(3):
                o_res[k, x, here, :] = res[k]
            for k in range(9):
                o_diag[k, x, here, :] = zero if entry_of[k] < 0 else diag[entry_of[k]]
            weights = prolong_of(cols, accum, x % 2 == 1, row_odd)
            for k in range(7):
                o_rows[k, x, here, :] = cols[k]
                o_pro[k, x, here, :] = weights[k]
            reduced = weight[0] * res[0] + weight[1] * res[1] + weight[2] * res[2]
            near, near_y = shares_of(weights, reduced, lanes)
            half = x // 2
            if x % 2 == 1:
                coarse[half, here, :] = near
                coarse_y[half, here, :] = near_y
                across = weights[4] * reduced
            else:
                coarse[half, here, :] = near + across
                coarse_y[half, here, :] = near_y
                coarse[half - 1, here, :] = coarse[half - 1, here, :] + weights[1] * reduced

        def send(k, src, dst):
            pltpu.make_async_copy(src, dst, sem.at[k, c]).start()

        for k, (src, dst) in enumerate(pieces(here)):
            send(k, src, dst)
        return carry

    def pieces(here):
        inner = pl.ds(1, span_x - 2)
        return [
            (o_res.at[:, inner, here], res_hbm.at[:, inner, here]),
            (o_diag.at[:, inner, here], diag_hbm.at[:, inner, here]),
            (o_rows.at[:, inner, here], rows_hbm.at[:, inner, here]),
            (o_pro.at[:, inner, here], pro_hbm.at[:, inner, here]),
            (o_low.at[0, :, pl.ds(1, span_x - 1), here], low_hbm.at[0, :, pl.ds(1, span_x - 1), here]),
            (o_up.at[0, :, pl.ds(0, span_x - 1), here], up_hbm.at[0, :, pl.ds(0, span_x - 1), here]),
            (o_low.at[pl.ds(1, 2), :, :, here], low_hbm.at[pl.ds(1, 2), :, :, here]),
            (o_up.at[pl.ds(1, 2), :, :, here], up_hbm.at[pl.ds(1, 2), :, :, here]),
        ]

    lax.fori_loop(0, chunks, chunk, 0)

    def drain(c, carry):
        here = pl.ds(pl.multiple_of(c * size, size), size)
        for k, (src, dst) in enumerate(pieces(here)):
            pltpu.make_async_copy(src, dst, sem.at[k, c]).wait()
        return carry

    lax.fori_loop(0, chunks, drain, 0)


def edge_kernel(
    part, mine_up, mine_dn, halo_lo, halo_hi, coarse_in, coarse_y_in,
    res_in, diag_in, low_in, up_in, rows_in, pro_in,
    res_hbm, diag_hbm, low_hbm, up_hbm, rows_hbm, pro_hbm, coarse, xev, xod, yev, yod,
    o_res, o_diag, o_blk, o_rows, o_pro, grid, grid_y, across, sem,
):
    span_y, lanes = mine_up.shape[1:]
    last_x = res_hbm.shape[1] - 1
    size = 8
    chunks = span_y // size
    pad = size
    row = lax.broadcasted_iota(jnp.int32, (size, lanes), 0)
    row_odd = row % 2 == 1
    zero = jnp.zeros((size, lanes), f32)
    for half in range(2):
        grid_y[half, 0:pad, :] = zero
        grid_y[half, pad + span_y : pad + span_y + pad, :] = zero

    def chunk(c, carry):
        base = pl.multiple_of(c * size, size)
        here = pl.ds(base, size)
        for side in range(2):
            res = [part[side, k, here, :] for k in range(3)]
            diag = [part[side, 3 + k, here, :] for k in range(distinct)]
            known = [part[side, 10 + k, here, :] for k in range(5)]
            accum = part[side, 15, here, :]
            cols = [None, known[0], known[1], known[2], known[0], known[3], known[4]]
            if side == 0:
                low = [halo_lo[k, here, :] for k in range(3)]
                high = [mine_dn[k, here, :] for k in range(7)]
            else:
                low = [mine_up[k, here, :] for k in range(3)]
                high = [halo_hi[k, here, :] for k in range(7)]
            flags = [a > 0.5 for a in high[4:]]
            flux, by_low, by_high = face(mobility_set(*low), mobility_set(*high[:3]), high[3], flags, head_flat)
            if side == 0:
                weight = weights_of(high[0])
                res = [a - b for a, b in zip(res, flux)]
                diag = [a - b for a, b in zip(diag, by_high)]
                block = [-v for v in by_low]
                cols[1] = column(weight, block)
            else:
                weight = weights_of(low[0])
                res = [a + b for a, b in zip(res, flux)]
                diag = [a + b for a, b in zip(diag, by_low)]
                block = by_high
                cols[4] = column(weight, block)
            cols[0] = column(weight, diag)
            for k in range(3):
                o_res[side, k, here, :] = res[k]
            for k in range(9):
                o_diag[side, k, here, :] = zero if entry_of[k] < 0 else diag[entry_of[k]]
                o_blk[side, k, here, :] = zero if entry_of[k] < 0 else block[entry_of[k]]
            weights = prolong_of(cols, accum, side == 1, row_odd)
            for k in range(7):
                o_rows[side, k, here, :] = cols[k]
                o_pro[side, k, here, :] = weights[k]
            reduced = weight[0] * res[0] + weight[1] * res[1] + weight[2] * res[2]
            near, near_y = shares_of(weights, reduced, lanes)
            grid[side, here, :] = coarse_in[side, here, :] + near
            grid_y[side, pl.ds(base + pad, size), :] = coarse_y_in[side, here, :] + near_y
            across[side, here, :] = weights[1 if side == 0 else 4] * reduced
        return carry

    lax.fori_loop(0, chunks, chunk, 0)
    copies = []

    def send(src, dst):
        copy = pltpu.make_async_copy(src, dst, sem.at[len(copies)])
        copy.start()
        copies.append(copy)

    for side, x in ((0, 0), (1, last_x)):
        send(o_res.at[side], res_hbm.at[:, x])
        send(o_diag.at[side], diag_hbm.at[:, x])
        send(o_blk.at[side], low_hbm.at[0, :, x] if side == 0 else up_hbm.at[0, :, x])
        send(o_rows.at[side], rows_hbm.at[:, x])
        send(o_pro.at[side], pro_hbm.at[:, x])
    half_y = span_y // 2
    gx_even = lax.axis_index("gx") % 2 == 0
    gy_even = lax.axis_index("gy") % 2 == 0
    down = across[0, pl.ds(0, half_y, 2), :] + across[0, pl.ds(1, half_y, 2), :]
    up = across[1, pl.ds(0, half_y, 2), :] + across[1, pl.ds(1, half_y, 2), :]
    xev[...] = jnp.where(gx_even, up, down)
    xod[...] = jnp.where(gx_even, down, up)
    for half in range(2):
        coarse[half] = (
            grid[half, pl.ds(0, half_y, 2), :]
            + grid[half, pl.ds(1, half_y, 2), :]
            + grid_y[half, pl.ds(pad + 2, half_y, 2), :]
            + grid_y[half, pl.ds(pad - 1, half_y, 2), :]
        )
        down = grid_y[half, pad : pad + 1, :]
        up = grid_y[half, pad + span_y - 1 : pad + span_y, :]
        yev[half : half + 1, :] = jnp.where(gy_even, up, down)
        yod[half : half + 1, :] = jnp.where(gy_even, down, up)
    for copy in copies:
        copy.wait()


def last_kernel(coarse, xev, xod, yev, yod, out):
    half_y = coarse.shape[1]
    gx_even = lax.axis_index("gx") % 2 == 0
    gy_even = lax.axis_index("gy") % 2 == 0
    out[0] = coarse[0] + jnp.where(gx_even, xod[...], xev[...])
    out[1] = coarse[1] + jnp.where(gx_even, xev[...], xod[...])
    low = jnp.where(gy_even, yod[...], yev[...])
    high = jnp.where(gy_even, yev[...], yod[...])
    for half in range(2):
        out[half, 0:1, :] = out[half, 0:1, :] + low[half : half + 1]
        out[half, half_y - 1 : half_y, :] = out[half, half_y - 1 : half_y, :] + high[half : half + 1]


def ring_of(axis, steps):
    count = lax.axis_size(axis)
    return [(i, (i + steps) % count) for i in range(count)]


def swap_of(axis, start):
    count = lax.axis_size(axis)
    pairs = []
    for i in range(start, count + start, 2):
        a, b = i % count, (i + 1) % count
        pairs += [(a, b), (b, a)]
    return pairs


hbm = pl.BlockSpec(memory_space=pl.ANY)
vmem = pl.BlockSpec(memory_space=pltpu.VMEM)


def shape_of(*shape):
    return jax.ShapeDtypeStruct(shape, f32)


def body(pressure, sat_water, sat_gas, pore_volume, mass_old, transmissibility, upwind):
    sx, sy, sz = pressure.shape
    xup, xdn, yev, yod = pl.pallas_call(
        pack_kernel,
        out_shape=[shape_of(3, sy, sz), shape_of(7, sy, sz), shape_of(7, sx, sz), shape_of(7, sx, sz)],
        in_specs=[hbm] * 5,
        out_specs=[vmem] * 4,
        scratch_shapes=[
            pltpu.VMEM((3, sx, 8, sz), f32),
            pltpu.VMEM((3, sx, 8, sz), f32),
            pltpu.VMEM((sx, 8, sz), f32),
            pltpu.VMEM((3, sx, 8, sz), jnp.int32),
            pltpu.VMEM((3, sy, sz), jnp.int32),
            pltpu.SemaphoreType.DMA((16,)),
        ],
        name="pack",
    )(pressure, sat_water, sat_gas, transmissibility, upwind)
    yev_in = lax.ppermute(yev, "gy", swap_of("gy", 0))
    yod_in = lax.ppermute(yod, "gy", swap_of("gy", 1))
    halo_hi = lax.ppermute(xdn, "gx", ring_of("gx", -1))
    halo_lo = lax.ppermute(xup, "gx", ring_of("gx", 1))
    outs = pl.pallas_call(
        main_kernel,
        out_shape=[
            shape_of(3, sx, sy, sz),
            shape_of(9, sx, sy, sz),
            shape_of(3, 9, sx, sy, sz),
            shape_of(3, 9, sx, sy, sz),
            shape_of(7, sx, sy, sz),
            shape_of(7, sx, sy, sz),
            shape_of(2, 16, sy, sz),
            shape_of(2, sy, sz),
            shape_of(2, sy, sz),
        ],
        in_specs=[vmem] * 9,
        out_specs=[hbm] * 6 + [vmem] * 3,
        scratch_shapes=[
            pltpu.VMEM((3, sx, sy, sz), f32),
            pltpu.VMEM((9, sx, sy, sz), f32),
            pltpu.VMEM((3, 9, sx, sy, sz), f32),
            pltpu.VMEM((3, 9, sx, sy, sz), f32),
            pltpu.VMEM((7, sx, sy, sz), f32),
            pltpu.VMEM((7, sx, sy, sz), f32),
            pltpu.VMEM((sx, 17, 16, sz), f32),
            pltpu.VMEM((3, sx, sz), f32),
            pltpu.SemaphoreType.DMA((8, sy // 8)),
        ],
        name="cells",
    )(pressure, sat_water, sat_gas, pore_volume, mass_old, transmissibility, upwind, yev_in, yod_in)
    big, (part, coarse, coarse_y) = outs[:6], outs[6:]
    outs = pl.pallas_call(
        edge_kernel,
        out_shape=[shape_of(*value.shape) for value in big]
        + [shape_of(2, sy // 2, sz), shape_of(sy // 2, sz), shape_of(sy // 2, sz), shape_of(2, sz), shape_of(2, sz)],
        in_specs=[vmem] * 7 + [hbm] * 6,
        out_specs=[hbm] * 6 + [vmem] * 5,
        input_output_aliases={7 + k: k for k in range(6)},
        scratch_shapes=[
            pltpu.VMEM((2, 3, sy, sz), f32),
            pltpu.VMEM((2, 9, sy, sz), f32),
            pltpu.VMEM((2, 9, sy, sz), f32),
            pltpu.VMEM((2, 7, sy, sz), f32),
            pltpu.VMEM((2, 7, sy, sz), f32),
            pltpu.VMEM((2, sy, sz), f32),
            pltpu.VMEM((2, sy + 16, sz), f32),
            pltpu.VMEM((2, sy, sz), f32),
            pltpu.SemaphoreType.DMA((10,)),
        ],
        name="edges",
    )(part, xup, xdn, halo_lo, halo_hi, coarse, coarse_y, *big)
    big, (coarse, xev, xod, yev, yod) = outs[:6], outs[6:]
    xev = lax.ppermute(xev, "gx", swap_of("gx", 0))
    xod = lax.ppermute(xod, "gx", swap_of("gx", 1))
    yev = lax.ppermute(yev, "gy", swap_of("gy", 0))
    yod = lax.ppermute(yod, "gy", swap_of("gy", 1))
    coarse = pl.pallas_call(
        last_kernel,
        out_shape=shape_of(2, sy // 2, sz),
        in_specs=[vmem] * 5,
        out_specs=vmem,
        name="finish",
    )(coarse, xev, xod, yev, yod)
    return (*big, coarse)


def solution(mesh):
    in_specs = (
        P("gx", "gy", None),
        P("gx", "gy", None),
        P("gx", "gy", None),
        P("gx", "gy", None),
        P(None, "gx", "gy", None),
        P(None, "gx", "gy", None),
        P(None, None, "gx", "gy", None),
    )
    out_specs = (
        P(None, "gx", "gy", None),
        P(None, "gx", "gy", None),
        P(None, None, "gx", "gy", None),
        P(None, None, "gx", "gy", None),
        P(None, "gx", "gy", None),
        P(None, "gx", "gy", None),
        P("gx", "gy", None),
    )
    return jax.shard_map(body, mesh=mesh, in_specs=in_specs, out_specs=out_specs, check_vma=False)
```
